32 devices in a mesh: slab: 2 (over y), row: 8 (over z, x), col: 2 (over core).
Axes of the slice: x: 2, y: 2, z: 4, core: 2. Of those that a mesh axis runs over, the one named last changes fastest.
Arguments:
- radiance: bfloat16 [16, 256, 256], P('slab', 'row', 'col'), parts along dimension 0, may hold values from -6 to 6
- sky_view: bfloat16 [32, 256, 256], P('slab', 'row', 'col'), parts along dimension 0, may hold values from 0.19921875 to 1
- tap_weight: float32 [33, 33], replicated, may hold values from 0.01 to 0.1
- tap_sector: int32 [33, 33], replicated, may hold values from 0 to 15
- far_weight: float32 [33, 33], replicated, may hold values from 0.08 to 0.8
- land_mask: int32 [16, 2], P(('slab', 'row'), 'col'), parts along dimension 0, may hold values 0 or 1
Outputs:
- reflected: bfloat16 [16, 256, 256], P('slab', 'row', 'col'), parts along dimension 0
The draws below stay inside these ranges and needn't reach their ends.
There are 2 independent parts, one for each index of `slab`. The reference program is written for one: setup_inputs(seed, part) draws one part's arguments, and reference() takes and returns one part's arrays. A program takes and returns all parts, laid end to end along the dimension named above; an argument that names none is the same for every part. Nothing has to cross between parts.
All inputs are finite; a program needn't handle non-finite values. No bound on the sum of `land_mask` on one device may be relied on, other than what follows from the above.
Results may differ from the reference program's by a relative error of at most 0.012.
Values may be sent and summed in bfloat16 or wider, within the bound.
No kernel may reach another device: no remote copies, remote signals or barrier semaphores. Data moves between devices by JAX's collectives and lax.ppermute only.
A program may use at most 64 MiB of HBM per device.

```python
import math
import jax
import jax.numpy as jnp
from jax import lax

B = 8
S = 16
RAD = 16
RC = 16
DEC = 16
CR = 32
CC = 128
NROWS = 256
NCOLS = 256
N_ROW = 8
N_COL = 2


def plant(entries, own_key, low, largest):
    longest = entries.shape.index(max(entries.shape))
    spots = []
    for shift in (0, 1):
        where = [jax.random.randint(jax.random.fold_in(own_key, axis), (), 0, length) for axis, length in enumerate(entries.shape)]
        where[longest] = (where[longest] + shift) % entries.shape[longest]
        spots.append(tuple(where))
    return entries.at[spots[0]].set(low).at[spots[1]].set(largest)


def level_of(rng, dims, cuts, low, high):
    gain, own = 1.0, jax.random.fold_in(rng, 6)
    for position, parts in cuts:
        steps = jnp.exp(jax.random.uniform(jax.random.fold_in(own, position), (parts,), jnp.float32, low / len(cuts), high / len(cuts)))
        gain = gain * jnp.repeat(steps, dims[position] // parts).reshape([-1 if axis == position else 1 for axis in range(len(dims))])
    return gain


def noise(key, extent, scale, reach, split=(), kind=jnp.bfloat16):
    array = scale * jax.random.normal(key, extent, jnp.float32)
    if split:
        array = array * level_of(key, extent, split, -0.22, 0.18)
    return jnp.clip(array, -reach, reach).astype(kind)


def setup_inputs(seed: int = 0, part: int = 0) -> dict:
    key_list = jax.random.split(jax.random.key(seed), 7)
    own_keys = jax.random.split(jax.random.fold_in(key_list[6], part), 7)
    return {
        "radiance": noise(own_keys[0], (B, NROWS, NCOLS), 1.0, 6.0, ((1, 8), (2, 2))),
        "sky_view": jnp.clip(0.19921875 + 0.80078125 * jax.random.uniform(own_keys[1], (S, NROWS, NCOLS), jnp.float32) ** level_of(own_keys[1], (S, NROWS, NCOLS), ((1, 8), (2, 2)), -0.2, 0.2), 0.19921875, 1.0).astype(jnp.bfloat16),
        "tap_weight": jnp.clip(jnp.exp(jax.random.uniform(key_list[2], (2 * RAD + 1, 2 * RAD + 1), jnp.float32, math.log(0.01), math.log(0.1))), 0.01, 0.1),
        "tap_sector": plant(jax.random.randint(key_list[3], (2 * RAD + 1, 2 * RAD + 1), 0, S), jax.random.fold_in(key_list[3], 1), 0, S - 1).astype(jnp.int32),
        "far_weight": jnp.clip(jnp.exp(jax.random.uniform(key_list[4], (2 * RC + 1, 2 * RC + 1), jnp.float32, math.log(0.08), math.log(0.8))), 0.08, 0.8),
        "land_mask": plant((jax.random.randint(own_keys[5], (N_ROW, N_COL), 0, 4) < 3).astype(jnp.int32), jax.random.fold_in(own_keys[5], 1), 0, 1),
    }


def reference(radiance, sky_view, tap_weight, tap_sector, far_weight, land_mask):
    sector_count = sky_view.shape[0]
    selector = tap_sector[None] == jnp.arange(sector_count, dtype=jnp.int32)[:, None, None]
    kernels = jnp.where(selector, tap_weight[None], 0.0).astype(jnp.bfloat16)[:, None]
    weights = sky_view.astype(jnp.float32)

    def per_band(plane):
        sector_sums = lax.conv_general_dilated(plane[None, None], kernels, (1, 1), [(RAD, RAD), (RAD, RAD)], preferred_element_type=jnp.float32)[0]
        return jnp.sum(sector_sums * weights, axis=0)

    near_field = lax.map(per_band, radiance)
    band_count, row_total, col_total = radiance.shape
    blocks = radiance.astype(jnp.float32).reshape(band_count, row_total // DEC, DEC, col_total // DEC, DEC)
    coarse = jnp.mean(blocks, axis=(2, 4)).astype(jnp.bfloat16)
    far_field = lax.conv_general_dilated(coarse.astype(jnp.float32)[:, None], far_weight[None, None], (1, 1), [(RC, RC), (RC, RC)], precision=lax.Precision.HIGHEST)[:, 0]
    far_fine = jnp.repeat(jnp.repeat(far_field, DEC, axis=1), DEC, axis=2)
    mask_fine = jnp.repeat(jnp.repeat(land_mask, CR, axis=0), CC, axis=1)
    total = jnp.where(mask_fine[None] > 0, near_field + far_fine, 0.0)
    return total.astype(jnp.bfloat16)
```

```python
import functools

import jax
import jax.numpy as jnp
from jax import lax
from jax.experimental import pallas as pl
from jax.experimental.pallas import tpu as pltpu
from jax.sharding import PartitionSpec as P

DEC = 16
STEP = 16
LANES = 128
F32 = jnp.float32
BF16 = jnp.bfloat16
I32 = jnp.int32


def iota(shape, axis):
    return lax.broadcasted_iota(I32, shape, axis)


def swap(value, axes, pairs):
    return lax.ppermute(value, axes, pairs)


def shifted(value, axis, steps):
    count = lax.axis_size(axis)
    leading, last = (max(0, -steps), min(count, count - steps))
    return lax.ppermute(value, axis, [(source, source + steps) for source in range(leading, last)])


def prepare_kernel(place_ref, radiance_ref, message_ref):
    row, col = place_ref[0], place_ref[1]
    bands, rows, cols = radiance_ref.shape
    cells = radiance_ref[...].reshape(bands * rows, cols)
    place = iota((cols, 256), 0) // DEC + col * (cols // DEC)
    chooser = (iota((cols, 256), 1) // 16 == place).astype(BF16)
    sums = jnp.dot(cells, chooser, preferred_element_type=F32)
    height = rows // DEC
    own_row = (iota((bands * rows, 256), 0) % rows) // DEC + row * height
    sums = jnp.where(iota((bands * rows, 256), 1) % 16 == own_row, sums, 0.0)
    coarse = jnp.sum(sums.reshape(bands, rows, 256), axis=1) * (1.0 / (DEC * DEC))
    coarse = jnp.concatenate([coarse[:, :LANES], coarse[:, LANES:]], axis=0)
    message_ref[rows : rows + 2 * bands, :] = coarse.astype(BF16)
    lane = iota((rows, cols), 1)
    packed = jnp.zeros((rows, cols), F32)
    for b in range(bands):
        moved = pltpu.roll(radiance_ref[b].astype(F32), 16 * b, 1)
        first = 16 * b - 16 * (1 - col)
        packed = jnp.where(((lane - first) & (cols - 1)) < 16, moved, packed)
    message_ref[0:rows, :] = packed.astype(BF16)


def pack_kernel(place_ref, radiance_ref, own_ref, side_ref, first_ref, second_ref):
    row = place_ref[0]
    bands, rows, cols = radiance_ref.shape
    odd = row & 1
    near = pl.multiple_of(STEP * (1 - odd), STEP)
    away = pl.multiple_of(STEP * odd, STEP)
    first_ref[0:bands] = radiance_ref[:, pl.ds(near, STEP), :]
    first_ref[bands] = side_ref[pl.ds(near, STEP), :]
    first_ref[bands + 1] = own_ref[rows : rows + 16, :] + side_ref[rows : rows + 16, :]
    second_ref[0:bands] = radiance_ref[:, pl.ds(away, STEP), :]
    second_ref[bands] = side_ref[pl.ds(away, STEP), :]


def weights_kernel(height, place_ref, tap_ref, sector_ref, far_ref, taps_ref, spread_ref, tap_s, far_s):
    row, col = place_ref[0], place_ref[1]
    span = tap_ref.shape[0]
    tall = span + STEP - 1
    wide = taps_ref.shape[1]
    sectors = taps_ref.shape[0] // STEP
    tap_s[...] = jnp.zeros(tap_s.shape, F32)
    tap_s[0:span, 0:span] = tap_ref[...]
    tap_s[tall : tall + span, 0:span] = sector_ref[...].astype(F32)
    lane = iota((LANES, wide), 1) - tall * iota((LANES, wide), 0)
    pick = ((lane >= 0) & (lane < tall)).astype(BF16)
    both = jnp.dot(tap_s[...].astype(BF16), pick, preferred_element_type=F32)
    which = iota((tall, wide), 1) % tall == iota((tall, wide), 0)
    weight = jnp.sum(jnp.where(which, both[0:tall], 0.0), axis=0, keepdims=True)
    sector = jnp.sum(jnp.where(which, both[tall:], 0.0), axis=0, keepdims=True)
    weight = pltpu.roll(jnp.broadcast_to(weight, (STEP, wide)), 0, 1, stride=1, stride_axis=0)
    sector = pltpu.roll(jnp.broadcast_to(sector, (STEP, wide)), 0, 1, stride=1, stride_axis=0)
    for s in range(sectors):
        taps_ref[s * STEP : (s + 1) * STEP, :] = jnp.where(sector == s, weight, 0.0).astype(BF16)
    far_s[...] = jnp.zeros(far_s.shape, F32)
    far_s[8 : 8 + span, 0:span] = far_ref[...]
    reach = (span - 1) // 2
    coarse_cols = LANES // DEC
    all_cols = spread_ref.shape[0] // (2 * height)
    lane = iota((LANES, all_cols * LANES), 1)
    want = lane // LANES - coarse_cols * col - (lane % LANES) // DEC + reach
    pick = (iota((LANES, all_cols * LANES), 0) == want).astype(BF16)
    parts = []
    for i in range(2):
        start = place_ref[3] - i + 8
        whole = far_s[pl.ds(start, height), :]
        high = whole.astype(BF16)
        low = (whole - high.astype(F32)).astype(BF16)
        parts += [high.astype(F32), low.astype(F32)]
    stacked = jnp.concatenate(parts, axis=0).astype(BF16)
    moved = jnp.dot(stacked, pick, preferred_element_type=F32).astype(BF16)
    for i in range(2):
        for part in range(2):
            rows = moved[(2 * i + part) * height : (2 * i + part + 1) * height]
            for J in range(all_cols):
                at = (part * all_cols + J) * height
                spread_ref[at : at + height, i * LANES : (i + 1) * LANES] = rows[:, J * LANES : (J + 1) * LANES]


def near_kernel(place_ref, taps_ref, radiance_ref, side_ref, first_ref, second_ref, sky_ref, near_ref, tiles):
    row, col, last = place_ref[0], place_ref[1], place_ref[4]
    bands, rows, cols = radiance_ref.shape
    sectors = sky_ref.shape[0]
    span = 33
    reach = 16
    tall = STEP + span - 1
    odd = (row & 1) == 1
    keep_up = row > 0
    keep_low = row < last
    tiles[:, span * tall :, :] = jnp.zeros((2, tiles.shape[1] - span * tall, tiles.shape[2]), BF16)
    zero = jnp.zeros((STEP, cols), F32)

    def around(b, middle):
        one = first_ref[b].astype(F32)
        two = second_ref[b].astype(F32)
        up = jnp.where(keep_up, jnp.where(odd, one, two), zero)
        low = jnp.where(keep_low, jnp.where(odd, two, one), zero)
        return jnp.concatenate([up, middle.astype(F32), low], axis=0)

    packed = around(bands, side_ref[0:rows, :])
    lane = iota(packed.shape, 1)
    edge = jnp.where(col == 0, (lane < reach).astype(F32), (lane >= cols - reach).astype(F32))
    for b in range(bands):
        own = around(b, radiance_ref[b])
        aux = pltpu.roll(packed, (cols - 16 * b) % cols, 1) * edge
        slot = b % 2
        for d in range(span):
            shift = d - reach
            if shift > 0:
                value = jnp.where(lane < shift, aux, own)
            elif shift < 0:
                value = jnp.where(lane >= cols + shift, aux, own)
            else:
                value = own
            if shift:
                value = pltpu.roll(value, (cols - shift) % cols, 1)
            value = value.astype(BF16)
            for i in range(2):
                tiles[slot, d * tall : (d + 1) * tall, i * cols : (i + 1) * cols] = value[i * STEP : i * STEP + tall]
        sums = jnp.dot(taps_ref[...], tiles[slot], preferred_element_type=F32)
        for i in range(2):
            part = sums[:, i * cols : (i + 1) * cols].reshape(sectors, STEP, cols)
            sky = sky_ref[:, i * STEP : (i + 1) * STEP, :].astype(F32)
            near_ref[b, i * STEP : (i + 1) * STEP, :] = jnp.sum(part * sky, axis=0)


def finish_kernel(place_ref, spread_ref, mine_ref, theirs_ref, near_ref, out_ref):
    bands = near_ref.shape[0]
    if mine_ref.shape[0] == 2 * bands:
        known = mine_ref[...].astype(F32) + theirs_ref[...].astype(F32)
        known = jnp.concatenate([known[:bands], known[bands:]], axis=1)
    else:
        known = mine_ref[...].astype(F32)
    known = jnp.concatenate([known, known], axis=1).astype(BF16)
    far = jnp.dot(known, spread_ref[...], preferred_element_type=F32)
    land = place_ref[2] > 0
    for i in range(2):
        block = far[:, i * LANES : (i + 1) * LANES][:, None, :]
        total = near_ref[:, i * DEC : (i + 1) * DEC, :] + block
        out_ref[:, i * DEC : (i + 1) * DEC, :] = jnp.where(land, total, 0.0).astype(BF16)


def call(kernel, out_shape, operands, scratch=(), flops=0):
    in_specs = [pl.BlockSpec(memory_space=pltpu.SMEM)]
    in_specs += [pl.BlockSpec(memory_space=pltpu.VMEM)] * (len(operands) - 1)
    moved = sum(a.size * a.dtype.itemsize for a in operands)
    return pl.pallas_call(
        kernel,
        out_shape=out_shape,
        in_specs=in_specs,
        out_specs=jax.tree.map(lambda _: pl.BlockSpec(memory_space=pltpu.VMEM), out_shape),
        scratch_shapes=list(scratch),
        compiler_params=pltpu.CompilerParams(vmem_limit_bytes=40 << 20),
        cost_estimate=pl.CostEstimate(flops=flops, bytes_accessed=moved, transcendentals=0),
    )(*operands)


def coarse_window(radiance, reach):
    bands, rows, cols = radiance.shape
    coarse_rows = rows // DEC
    hops = reach // coarse_rows
    live = min(hops, lax.axis_size("row") - 1)
    blocks = radiance.astype(F32).reshape(bands, coarse_rows, DEC, cols // DEC, DEC)
    own = jnp.mean(blocks, axis=(2, 4)).astype(BF16)
    pieces = [jnp.zeros_like(own)] * (2 * hops + 1)
    pieces[hops] = own
    lower = upper = own
    for k in range(1, live + 1):
        lower = shifted(lower, "row", 1)
        upper = shifted(upper, "row", -1)
        pieces[hops - k] = lower
        pieces[hops + k] = upper
    band = jnp.concatenate(pieces, axis=1)
    band = lax.all_gather(band, "col", axis=2, tiled=True)
    return jnp.transpose(band, (0, 2, 1))


def body(radiance, sky_view, tap_weight, tap_sector, far_weight, land_mask):
    bands, rows, cols = radiance.shape
    sectors = sky_view.shape[0]
    span = tap_weight.shape[0]
    far_reach = (far_weight.shape[0] - 1) // 2
    n_row, n_col = lax.axis_size("row"), lax.axis_size("col")
    coarse_rows = rows // DEC
    compact = n_row & (n_row - 1) == 0 and n_row * coarse_rows == 16
    all_cols = n_col * cols // DEC
    row, col = lax.axis_index("row"), lax.axis_index("col")
    start = far_reach - coarse_rows * row if compact else 0 * row
    place = jnp.stack([row, col, land_mask[0, 0], start, 0 * row + n_row - 1]).astype(I32)

    def shape(*dims, kind=BF16):
        return jax.ShapeDtypeStruct(dims, kind)

    message = call(prepare_kernel, shape(rows + 16, LANES), [place, radiance])
    side = swap(message, "col", [(0, 1), (1, 0)])
    first, second = call(
        pack_kernel,
        (shape(bands + 2, STEP, LANES), shape(bands + 1, STEP, LANES)),
        [place, radiance, message, side],
    )

    def flat(r, c):
        return r * n_col + c

    def other(r, c):
        q = r + 1 if r % 2 else r - 1
        return flat(q, c) if 0 <= q < n_row else flat(r, 1 - c)

    everyone = [(r, c) for r in range(n_row) for c in range(n_col)]
    from_first = swap(first, "row", [(r, r ^ 1) for r in range(n_row)])

    height = 16 if compact else 48
    tall = span + STEP - 1
    wide = -(-span * tall // LANES) * LANES
    taps, spread = call(
        functools.partial(weights_kernel, height),
        (shape(sectors * STEP, wide), shape(2 * all_cols * height, 2 * LANES)),
        [place, tap_weight, tap_sector, far_weight],
        [pltpu.VMEM((2 * tall, LANES), F32), pltpu.VMEM((64, LANES), F32)],
        flops=10_000_000,
    )

    if compact:
        known = first[bands + 1] + from_first[bands + 1]
        known, second = lax.optimization_barrier((known, second))
        theirs = swap(known, "row", [(r, r ^ 2) for r in range(n_row)])
        from_second = swap(second, ("row", "col"), [(flat(r, c), other(r, c)) for r, c in everyone])
        step = 4
        while step < n_row:
            known = known + theirs
            theirs = swap(known, "row", [(r, r ^ step) for r in range(n_row)])
            step *= 2
    else:
        from_second = swap(second, ("row", "col"), [(flat(r, c), other(r, c)) for r, c in everyone])
        window = coarse_window(radiance, far_reach)
        window = jnp.pad(window, ((0, 0), (0, 0), (0, height - window.shape[2])))
        known = theirs = window.reshape(bands, all_cols * height)

    near = call(
        near_kernel,
        shape(bands, rows, cols, kind=F32),
        [place, taps, radiance, side, from_first, from_second, sky_view],
        [pltpu.VMEM((2, wide, 2 * cols), BF16)],
        flops=2 * sectors * STEP * wide * 2 * cols * bands,
    )
    return call(finish_kernel, shape(bands, rows, cols), [place, spread, known, theirs, near])


def solution(mesh):
    in_specs = (
        P("slab", "row", "col"),
        P("slab", "row", "col"),
        P(),
        P(),
        P(),
        P(("slab", "row"), "col"),
    )
    out_specs = P("slab", "row", "col")
    return jax.shard_map(body, mesh=mesh, in_specs=in_specs, out_specs=out_specs, check_vma=False)
```

```python
import functools

import jax
import jax.numpy as jnp
from jax import lax
from jax.experimental import pallas as pl
from jax.experimental.pallas import tpu as pltpu
from jax.sharding import PartitionSpec as P

DEC = 16
STEP = 16
LANES = 128
F32 = jnp.float32
BF16 = jnp.bfloat16
I32 = jnp.int32


def iota(shape, axis):
    return lax.broadcasted_iota(I32, shape, axis)


def swap(value, axes, pairs):
    return lax.ppermute(value, axes, pairs)


def shifted(value, axis, steps):
    count = lax.axis_size(axis)
    leading, last = (max(0, -steps), min(count, count - steps))
    return lax.ppermute(value, axis, [(source, source + steps) for source in range(leading, last)])


def prepare_kernel(radiance_ref, message_ref):
    row, col = lax.axis_index("row"), lax.axis_index("col")
    bands, rows, cols = radiance_ref.shape
    height = rows // DEC
    cells = radiance_ref[...].reshape(bands * rows, cols)
    place = (iota((cols, 256), 0) >> 4) + col * (cols // DEC)
    chooser = ((iota((cols, 256), 1) >> 4) == place).astype(BF16)
    sums = jnp.dot(cells, chooser, preferred_element_type=F32)
    sums = jnp.sum(sums.reshape(bands, height, DEC, 256), axis=2)
    own_row = (iota((bands, height, 256), 2) & 15) - iota((bands, height, 256), 1)
    coarse = jnp.sum(jnp.where(own_row == row * height, sums, 0.0), axis=1) * (1.0 / (DEC * DEC))
    coarse = jnp.concatenate([coarse[:, :LANES], coarse[:, LANES:]], axis=0)
    message_ref[rows : rows + 2 * bands, :] = coarse.astype(BF16)
    lane = iota((rows, cols), 1)
    packed = jnp.zeros((rows, cols), F32)
    for b in range(bands):
        moved = pltpu.roll(radiance_ref[b].astype(F32), 16 * b, 1)
        first = 16 * b - 16 * (1 - col)
        packed = jnp.where(((lane - first) & (cols - 1)) < 16, moved, packed)
    message_ref[0:rows, :] = packed.astype(BF16)


def pack_kernel(radiance_ref, own_ref, side_ref, first_ref, second_ref):
    bands, rows, cols = radiance_ref.shape
    odd = lax.axis_index("row") & 1
    near = pl.multiple_of(STEP * (1 - odd), STEP)
    away = pl.multiple_of(STEP * odd, STEP)
    first_ref[0:bands] = radiance_ref[:, pl.ds(near, STEP), :]
    first_ref[bands] = side_ref[pl.ds(near, STEP), :]
    first_ref[bands + 1] = own_ref[rows : rows + 16, :] + side_ref[rows : rows + 16, :]
    second_ref[0:bands] = radiance_ref[:, pl.ds(away, STEP), :]
    second_ref[bands] = side_ref[pl.ds(away, STEP), :]


def weights_kernel(
    height, whole_grid, land_ref, tap_ref, sector_ref, far_ref, sky_ref, taps_ref, spread_ref, view_ref, tap_s, far_s, sky_s, sem
):
    row, col = lax.axis_index("row"), lax.axis_index("col")
    fetch = pltpu.make_async_copy(sky_ref, sky_s, sem)
    fetch.start()
    land = land_ref[0, 0] > 0
    span = tap_ref.shape[0]
    tall = span + STEP - 1
    wide = taps_ref.shape[1]
    sectors = taps_ref.shape[0] // STEP
    tap_s[...] = jnp.zeros(tap_s.shape, F32)
    tap_s[0:span, 0:span] = tap_ref[...]
    tap_s[tall : tall + span, 0:span] = sector_ref[...].astype(F32)
    lane = iota((LANES, wide), 1) - tall * iota((LANES, wide), 0)
    pick = ((lane >= 0) & (lane < tall)).astype(BF16)
    both = jnp.dot(tap_s[...].astype(BF16), pick, preferred_element_type=F32)
    which = iota((tall, wide), 1) % tall == iota((tall, wide), 0)
    weight = jnp.sum(jnp.where(which, both[0:tall], 0.0), axis=0, keepdims=True)
    sector = jnp.sum(jnp.where(which, both[tall:], 0.0), axis=0, keepdims=True)
    weight = pltpu.roll(jnp.broadcast_to(weight, (STEP, wide)), 0, 1, stride=1, stride_axis=0)
    sector = pltpu.roll(jnp.broadcast_to(sector, (STEP, wide)), 0, 1, stride=1, stride_axis=0)
    for s in range(sectors):
        taps_ref[s * STEP : (s + 1) * STEP, :] = jnp.where(sector == s, weight, 0.0).astype(BF16)
    far_s[...] = jnp.zeros(far_s.shape, F32)
    far_s[8 : 8 + span, 0:span] = far_ref[...]
    reach = (span - 1) // 2
    coarse_cols = LANES // DEC
    all_cols = spread_ref.shape[0] // (2 * height)
    lane = iota((LANES, all_cols * LANES), 1)
    want = (lane >> 7) - coarse_cols * col - ((lane & (LANES - 1)) >> 4) + reach
    pick = ((iota((LANES, all_cols * LANES), 0) == want) & land).astype(BF16)
    parts = []
    for i in range(2):
        start = (reach - 2 * row if whole_grid else 0) - i + 8
        whole = far_s[pl.ds(start, height), :]
        high = whole.astype(BF16)
        low = (whole - high.astype(F32)).astype(BF16)
        parts += [high.astype(F32), low.astype(F32)]
    stacked = jnp.concatenate(parts, axis=0).astype(BF16)
    moved = jnp.dot(stacked, pick, preferred_element_type=F32).astype(BF16)
    for i in range(2):
        for part in range(2):
            rows = moved[(2 * i + part) * height : (2 * i + part + 1) * height]
            for J in range(all_cols):
                at = (part * all_cols + J) * height
                spread_ref[at : at + height, i * LANES : (i + 1) * LANES] = rows[:, J * LANES : (J + 1) * LANES]
    fetch.wait()
    view_ref[...] = jnp.where(land, sky_s[...].astype(F32), 0.0)


def near_kernel(offset, taps_ref, radiance_ref, side_ref, first_ref, second_ref, sky_ref, near_ref, tiles):
    row, col, last = lax.axis_index("row"), lax.axis_index("col"), lax.axis_size("row") - 1
    bands, rows, cols = radiance_ref.shape
    sectors = sky_ref.shape[0]
    span = 33
    reach = 16
    tall = STEP + span - 1
    odd = (row & 1) == 1
    keep_up = row > 0
    keep_low = row < last
    tiles[:, span * tall :, :] = jnp.zeros((2, tiles.shape[1] - span * tall, tiles.shape[2]), BF16)
    zero = jnp.zeros((STEP, cols), F32)

    def around(b, middle):
        one = first_ref[b].astype(F32)
        two = second_ref[b].astype(F32)
        up = jnp.where(keep_up, jnp.where(odd, one, two), zero)
        low = jnp.where(keep_low, jnp.where(odd, two, one), zero)
        return jnp.concatenate([up, middle.astype(F32), low], axis=0)

    packed = around(bands, side_ref[0:rows, :])
    lane = iota(packed.shape, 1)
    edge = jnp.where(col == 0, (lane < reach).astype(F32), (lane >= cols - reach).astype(F32))
    for n in range(near_ref.shape[0]):
        b = offset + n
        own = around(b, radiance_ref[b])
        aux = pltpu.roll(packed, (cols - 16 * b) % cols, 1) * edge
        slot = n % 2
        for d in range(span):
            shift = d - reach
            if shift > 0:
                value = jnp.where(lane < shift, aux, own)
            elif shift < 0:
                value = jnp.where(lane >= cols + shift, aux, own)
            else:
                value = own
            if shift:
                value = pltpu.roll(value, (cols - shift) % cols, 1)
            value = value.astype(BF16)
            for i in range(2):
                tiles[slot, d * tall : (d + 1) * tall, i * cols : (i + 1) * cols] = value[i * STEP : i * STEP + tall]
        sums = jnp.dot(taps_ref[...], tiles[slot], preferred_element_type=F32)
        for i in range(2):
            part = sums[:, i * cols : (i + 1) * cols].reshape(sectors, STEP, cols)
            sky = sky_ref[:, i * STEP : (i + 1) * STEP, :]
            near_ref[n, i * STEP : (i + 1) * STEP, :] = jnp.sum(part * sky, axis=0)


def finish_kernel(spread_ref, mine_ref, theirs_ref, *rest):
    near_refs, out_ref = rest[:-1], rest[-1]
    bands = out_ref.shape[0]
    if mine_ref.shape[0] == 2 * bands:
        known = mine_ref[...].astype(F32) + theirs_ref[...].astype(F32)
        known = jnp.concatenate([known[:bands], known[bands:]], axis=1)
    else:
        known = mine_ref[...].astype(F32)
    known = jnp.concatenate([known, known], axis=1).astype(BF16)
    far = jnp.dot(known, spread_ref[...], preferred_element_type=F32)
    at = 0
    for near_ref in near_refs:
        count = near_ref.shape[0]
        for i in range(2):
            block = far[at : at + count, i * LANES : (i + 1) * LANES][:, None, :]
            total = near_ref[:, i * DEC : (i + 1) * DEC, :] + block
            out_ref[at : at + count, i * DEC : (i + 1) * DEC, :] = total.astype(BF16)
        at += count


VMEM = pl.BlockSpec(memory_space=pltpu.VMEM)
SMEM = pl.BlockSpec(memory_space=pltpu.SMEM)
HBM = pl.BlockSpec(memory_space=pl.ANY)


def call(kernel, out_shape, operands, scratch=(), flops=0, in_specs=None):
    moved = sum(a.size * a.dtype.itemsize for a in operands)
    return pl.pallas_call(
        kernel,
        out_shape=out_shape,
        in_specs=in_specs or [VMEM] * len(operands),
        out_specs=jax.tree.map(lambda _: VMEM, out_shape),
        scratch_shapes=list(scratch),
        compiler_params=pltpu.CompilerParams(vmem_limit_bytes=40 << 20),
        cost_estimate=pl.CostEstimate(flops=flops, bytes_accessed=moved, transcendentals=0),
    )(*operands)


def coarse_window(radiance, reach):
    bands, rows, cols = radiance.shape
    coarse_rows = rows // DEC
    hops = reach // coarse_rows
    live = min(hops, lax.axis_size("row") - 1)
    blocks = radiance.astype(F32).reshape(bands, coarse_rows, DEC, cols // DEC, DEC)
    own = jnp.mean(blocks, axis=(2, 4)).astype(BF16)
    pieces = [jnp.zeros_like(own)] * (2 * hops + 1)
    pieces[hops] = own
    lower = upper = own
    for k in range(1, live + 1):
        lower = shifted(lower, "row", 1)
        upper = shifted(upper, "row", -1)
        pieces[hops - k] = lower
        pieces[hops + k] = upper
    band = jnp.concatenate(pieces, axis=1)
    band = lax.all_gather(band, "col", axis=2, tiled=True)
    return jnp.transpose(band, (0, 2, 1))


def body(radiance, sky_view, tap_weight, tap_sector, far_weight, land_mask):
    bands, rows, cols = radiance.shape
    sectors = sky_view.shape[0]
    span = tap_weight.shape[0]
    far_reach = (far_weight.shape[0] - 1) // 2
    n_row, n_col = lax.axis_size("row"), lax.axis_size("col")
    coarse_rows = rows // DEC
    compact = n_row & (n_row - 1) == 0 and n_row * coarse_rows == 16
    all_cols = n_col * cols // DEC

    def shape(*dims, kind=BF16):
        return jax.ShapeDtypeStruct(dims, kind)

    message = call(prepare_kernel, shape(rows + 16, LANES), [radiance])
    side = swap(message, "col", [(0, 1), (1, 0)])
    first, second = call(
        pack_kernel,
        (shape(bands + 2, STEP, LANES), shape(bands + 1, STEP, LANES)),
        [radiance, message, side],
    )

    def flat(r, c):
        return r * n_col + c

    def other(r, c):
        q = r + 1 if r % 2 else r - 1
        return flat(q, c) if 0 <= q < n_row else flat(r, 1 - c)

    everyone = [(r, c) for r in range(n_row) for c in range(n_col)]
    from_first = swap(first, "row", [(r, r ^ 1) for r in range(n_row)])
    from_second = swap(second, ("row", "col"), [(flat(r, c), other(r, c)) for r, c in everyone])

    height = 16 if compact else 48
    tall = span + STEP - 1
    wide = -(-span * tall // LANES) * LANES
    taps, spread, sky = call(
        functools.partial(weights_kernel, height, compact),
        (shape(sectors * STEP, wide), shape(2 * all_cols * height, 2 * LANES), shape(sectors, rows, cols, kind=F32)),
        [land_mask, tap_weight, tap_sector, far_weight, sky_view],
        [
            pltpu.VMEM((2 * tall, LANES), F32),
            pltpu.VMEM((64, LANES), F32),
            pltpu.VMEM(sky_view.shape, BF16),
            pltpu.SemaphoreType.DMA,
        ],
        in_specs=[SMEM, VMEM, VMEM, VMEM, HBM],
        flops=10_000_000,
    )

    def near(at, count):
        return call(
            functools.partial(near_kernel, at),
            shape(count, rows, cols, kind=F32),
            [taps, radiance, side, from_first, from_second, sky],
            [pltpu.VMEM((2, wide, 2 * cols), BF16)],
            flops=2 * sectors * STEP * wide * 2 * cols * count,
        )

    half = bands // 2
    if compact:
        from_first, taps, spread, sky = lax.optimization_barrier((from_first, taps, spread, sky))
        known = first[bands + 1] + from_first[bands + 1]
        theirs = swap(known, "row", [(r, r ^ 2) for r in range(n_row)])
        near_one = near(0, half)
        theirs, near_one = lax.optimization_barrier((theirs, near_one))
        step = 4
        while step < n_row:
            known = known + theirs
            theirs = swap(known, "row", [(r, r ^ step) for r in range(n_row)])
            step *= 2
    else:
        near_one = near(0, half)
        window = coarse_window(radiance, far_reach)
        window = jnp.pad(window, ((0, 0), (0, 0), (0, height - window.shape[2])))
        known = theirs = window.reshape(bands, all_cols * height)
    near_two = near(half, bands - half)
    return call(finish_kernel, shape(bands, rows, cols), [spread, known, theirs, near_one, near_two])


def solution(mesh):
    in_specs = (
        P("slab", "row", "col"),
        P("slab", "row", "col"),
        P(),
        P(),
        P(),
        P(("slab", "row"), "col"),
    )
    out_specs = P("slab", "row", "col")
    return jax.shard_map(body, mesh=mesh, in_specs=in_specs, out_specs=out_specs, check_vma=False)
```

```python
import functools

import jax
import jax.numpy as jnp
from jax import lax
from jax.experimental import pallas as pl
from jax.experimental.pallas import tpu as pltpu
from jax.sharding import PartitionSpec as P

DEC = 16
STEP = 16
LANES = 128
F32 = jnp.float32
BF16 = jnp.bfloat16
I32 = jnp.int32


def iota(shape, axis):
    return lax.broadcasted_iota(I32, shape, axis)


def swap(value, axes, pairs):
    return lax.ppermute(value, axes, pairs)


def shifted(value, axis, steps):
    count = lax.axis_size(axis)
    leading, last = (max(0, -steps), min(count, count - steps))
    return lax.ppermute(value, axis, [(source, source + steps) for source in range(leading, last)])


def prepare_kernel(radiance, tap, sector, far, message_ref, radiance_ref, tap_ref, sector_ref, far_ref, sems):
    pairs = [(radiance, radiance_ref), (tap, tap_ref), (sector, sector_ref), (far, far_ref)]
    fetches = [pltpu.make_async_copy(*pair, sems.at[k]) for k, pair in enumerate(pairs)]
    for fetch in fetches:
        fetch.start()
    row, col = lax.axis_index("row"), lax.axis_index("col")
    bands, rows, cols = radiance_ref.shape
    fetches[0].wait()
    height = rows // DEC
    cells = radiance_ref[...].reshape(bands * rows, cols)
    place = (iota((cols, 256), 0) >> 4) + col * (cols // DEC)
    chooser = ((iota((cols, 256), 1) >> 4) == place).astype(BF16)
    sums = jnp.dot(cells, chooser, preferred_element_type=F32)
    sums = jnp.sum(sums.reshape(bands, height, DEC, 256), axis=2)
    own_row = (iota((bands, height, 256), 2) & 15) - iota((bands, height, 256), 1)
    coarse = jnp.sum(jnp.where(own_row == row * height, sums, 0.0), axis=1) * (1.0 / (DEC * DEC))
    coarse = jnp.concatenate([coarse[:, :LANES], coarse[:, LANES:]], axis=0)
    message_ref[rows : rows + 2 * bands, :] = coarse.astype(BF16)
    lane = iota((rows, cols), 1)
    packed = jnp.zeros((rows, cols), F32)
    for b in range(bands):
        moved = pltpu.roll(radiance_ref[b].astype(F32), 16 * b, 1)
        first = 16 * b - 16 * (1 - col)
        packed = jnp.where(((lane - first) & (cols - 1)) < 16, moved, packed)
    message_ref[0:rows, :] = packed.astype(BF16)
    for fetch in fetches[1:]:
        fetch.wait()


def pack_kernel(land_ref, radiance_ref, own_ref, side_ref, first_ref, second_ref, keep_ref):
    bands, rows, cols = radiance_ref.shape
    odd = lax.axis_index("row") & 1
    near = pl.multiple_of(STEP * (1 - odd), STEP)
    away = pl.multiple_of(STEP * odd, STEP)
    first_ref[0:bands] = radiance_ref[:, pl.ds(near, STEP), :]
    first_ref[bands] = side_ref[pl.ds(near, STEP), :]
    first_ref[bands + 1] = own_ref[rows : rows + 16, :] + side_ref[rows : rows + 16, :]
    second_ref[0:bands] = radiance_ref[:, pl.ds(away, STEP), :]
    second_ref[bands] = side_ref[pl.ds(away, STEP), :]
    ones = jnp.ones(keep_ref.shape, F32)
    keep_ref[...] = jnp.where(land_ref[0, 0] > 0, ones, jnp.zeros_like(ones))


def weights_kernel(
    height, whole_grid, tap_ref, sector_ref, far_ref, sky_ref, taps_ref, spread_ref, view_ref, tap_s, far_s
):
    row, col = lax.axis_index("row"), lax.axis_index("col")
    span = tap_ref.shape[0]
    tall = span + STEP - 1
    wide = taps_ref.shape[1]
    sectors = taps_ref.shape[0] // STEP
    tap_s[...] = jnp.zeros(tap_s.shape, F32)
    tap_s[0:span, 0:span] = tap_ref[...]
    tap_s[tall : tall + span, 0:span] = sector_ref[...].astype(F32)
    lane = iota((LANES, wide), 1) - tall * iota((LANES, wide), 0)
    pick = ((lane >= 0) & (lane < tall)).astype(BF16)
    both = jnp.dot(tap_s[...].astype(BF16), pick, preferred_element_type=F32)
    which = iota((tall, wide), 1) % tall == iota((tall, wide), 0)
    weight = jnp.sum(jnp.where(which, both[0:tall], 0.0), axis=0, keepdims=True)
    sector = jnp.sum(jnp.where(which, both[tall:], 0.0), axis=0, keepdims=True)
    weight = pltpu.roll(jnp.broadcast_to(weight, (STEP, wide)), 0, 1, stride=1, stride_axis=0)
    sector = pltpu.roll(jnp.broadcast_to(sector, (STEP, wide)), 0, 1, stride=1, stride_axis=0)
    for s in range(sectors):
        taps_ref[s * STEP : (s + 1) * STEP, :] = jnp.where(sector == s, weight, 0.0).astype(BF16)
    far_s[...] = jnp.zeros(far_s.shape, F32)
    far_s[8 : 8 + span, 0:span] = far_ref[...]
    reach = (span - 1) // 2
    coarse_cols = LANES // DEC
    all_cols = spread_ref.shape[0] // (2 * height)
    lane = iota((LANES, all_cols * LANES), 1)
    want = (lane >> 7) - coarse_cols * col - ((lane & (LANES - 1)) >> 4) + reach
    pick = (iota((LANES, all_cols * LANES), 0) == want).astype(BF16)
    parts = []
    for i in range(2):
        start = (reach - 2 * row if whole_grid else 0) - i + 8
        whole = far_s[pl.ds(start, height), :]
        high = whole.astype(BF16)
        low = (whole - high.astype(F32)).astype(BF16)
        parts += [high.astype(F32), low.astype(F32)]
    stacked = jnp.concatenate(parts, axis=0).astype(BF16)
    moved = jnp.dot(stacked, pick, preferred_element_type=F32).astype(BF16)
    for i in range(2):
        for part in range(2):
            rows = moved[(2 * i + part) * height : (2 * i + part + 1) * height]
            for J in range(all_cols):
                at = (part * all_cols + J) * height
                spread_ref[at : at + height, i * LANES : (i + 1) * LANES] = rows[:, J * LANES : (J + 1) * LANES]
    view_ref[...] = sky_ref[...].astype(F32)


def near_kernel(offset, taps_ref, radiance_ref, side_ref, first_ref, second_ref, sky_ref, near_ref, tiles):
    row, col, last = lax.axis_index("row"), lax.axis_index("col"), lax.axis_size("row") - 1
    bands, rows, cols = radiance_ref.shape
    sectors = sky_ref.shape[0]
    span = 33
    reach = 16
    tall = STEP + span - 1
    odd = (row & 1) == 1
    keep_up = row > 0
    keep_low = row < last
    tiles[:, span * tall :, :] = jnp.zeros((2, tiles.shape[1] - span * tall, tiles.shape[2]), BF16)
    zero = jnp.zeros((STEP, cols), F32)

    def around(b, middle):
        one = first_ref[b].astype(F32)
        two = second_ref[b].astype(F32)
        up = jnp.where(keep_up, jnp.where(odd, one, two), zero)
        low = jnp.where(keep_low, jnp.where(odd, two, one), zero)
        return jnp.concatenate([up, middle.astype(F32), low], axis=0)

    packed = around(bands, side_ref[0:rows, :])
    lane = iota(packed.shape, 1)
    edge = jnp.where(col == 0, (lane < reach).astype(F32), (lane >= cols - reach).astype(F32))
    for n in range(near_ref.shape[0]):
        b = offset + n
        own = around(b, radiance_ref[b])
        aux = pltpu.roll(packed, (cols - 16 * b) % cols, 1) * edge
        slot = n % 2
        for d in range(span):
            shift = d - reach
            if shift > 0:
                value = jnp.where(lane < shift, aux, own)
            elif shift < 0:
                value = jnp.where(lane >= cols + shift, aux, own)
            else:
                value = own
            if shift:
                value = pltpu.roll(value, (cols - shift) % cols, 1)
            value = value.astype(BF16)
            for i in range(2):
                tiles[slot, d * tall : (d + 1) * tall, i * cols : (i + 1) * cols] = value[i * STEP : i * STEP + tall]
        sums = jnp.dot(taps_ref[...], tiles[slot], preferred_element_type=F32)
        for i in range(2):
            part = sums[:, i * cols : (i + 1) * cols].reshape(sectors, STEP, cols)
            sky = sky_ref[:, i * STEP : (i + 1) * STEP, :]
            near_ref[n, i * STEP : (i + 1) * STEP, :] = jnp.sum(part * sky, axis=0)


def finish_kernel(keep_ref, spread_ref, mine_ref, theirs_ref, *rest):
    near_refs, out_ref = rest[:-1], rest[-1]
    bands = out_ref.shape[0]
    land = keep_ref[0:1, :] > 0
    if mine_ref.shape[0] == 2 * bands:
        known = mine_ref[...].astype(F32) + theirs_ref[...].astype(F32)
        known = jnp.concatenate([known[:bands], known[bands:]], axis=1)
    else:
        known = mine_ref[...].astype(F32)
    known = jnp.concatenate([known, known], axis=1).astype(BF16)
    far = jnp.dot(known, spread_ref[...], preferred_element_type=F32)
    at = 0
    for near_ref in near_refs:
        count = near_ref.shape[0]
        for i in range(2):
            block = far[at : at + count, i * LANES : (i + 1) * LANES][:, None, :]
            total = near_ref[:, i * DEC : (i + 1) * DEC, :] + block
            out_ref[at : at + count, i * DEC : (i + 1) * DEC, :] = jnp.where(land, total, 0.0).astype(BF16)
        at += count


VMEM = pl.BlockSpec(memory_space=pltpu.VMEM)
SMEM = pl.BlockSpec(memory_space=pltpu.SMEM)
HBM = pl.BlockSpec(memory_space=pltpu.HBM)


def call(kernel, out_shape, operands, scratch=(), flops=0, in_specs=None, vmem=40 << 20):
    moved = sum(a.size * a.dtype.itemsize for a in operands)
    return pl.pallas_call(
        kernel,
        out_shape=out_shape,
        in_specs=in_specs or [VMEM] * len(operands),
        out_specs=jax.tree.map(lambda _: VMEM, out_shape),
        scratch_shapes=list(scratch),
        compiler_params=pltpu.CompilerParams(vmem_limit_bytes=vmem),
        cost_estimate=pl.CostEstimate(flops=flops, bytes_accessed=moved, transcendentals=0),
    )(*operands)


def coarse_window(radiance, reach):
    bands, rows, cols = radiance.shape
    coarse_rows = rows // DEC
    hops = reach // coarse_rows
    live = min(hops, lax.axis_size("row") - 1)
    blocks = radiance.astype(F32).reshape(bands, coarse_rows, DEC, cols // DEC, DEC)
    own = jnp.mean(blocks, axis=(2, 4)).astype(BF16)
    pieces = [jnp.zeros_like(own)] * (2 * hops + 1)
    pieces[hops] = own
    lower = upper = own
    for k in range(1, live + 1):
        lower = shifted(lower, "row", 1)
        upper = shifted(upper, "row", -1)
        pieces[hops - k] = lower
        pieces[hops + k] = upper
    band = jnp.concatenate(pieces, axis=1)
    band = lax.all_gather(band, "col", axis=2, tiled=True)
    return jnp.transpose(band, (0, 2, 1))


def body(radiance, sky_view, tap_weight, tap_sector, far_weight, land_mask):
    bands, rows, cols = radiance.shape
    sectors = sky_view.shape[0]
    span = tap_weight.shape[0]
    far_reach = (far_weight.shape[0] - 1) // 2
    n_row, n_col = lax.axis_size("row"), lax.axis_size("col")
    coarse_rows = rows // DEC
    compact = n_row & (n_row - 1) == 0 and n_row * coarse_rows == 16
    all_cols = n_col * cols // DEC

    def shape(*dims, kind=BF16):
        return jax.ShapeDtypeStruct(dims, kind)

    inputs = [radiance, tap_weight, tap_sector, far_weight]
    message, radiance, tap_weight, tap_sector, far_weight = call(
        prepare_kernel,
        [shape(rows + 16, LANES)] + [jax.ShapeDtypeStruct(a.shape, a.dtype) for a in inputs],
        [pltpu.with_memory_space_constraint(a, pltpu.HBM) for a in inputs],
        [pltpu.SemaphoreType.DMA((len(inputs),))],
        in_specs=[HBM] * len(inputs),
    )
    side = swap(message, "col", [(0, 1), (1, 0)])
    first, second, keep = call(
        pack_kernel,
        (shape(bands + 2, STEP, LANES), shape(bands + 1, STEP, LANES), shape(8, LANES, kind=F32)),
        [land_mask, radiance, message, side],
        in_specs=[SMEM] + [VMEM] * 3,
    )

    def flat(r, c):
        return r * n_col + c

    def other(r, c):
        q = r + 1 if r % 2 else r - 1
        return flat(q, c) if 0 <= q < n_row else flat(r, 1 - c)

    everyone = [(r, c) for r in range(n_row) for c in range(n_col)]
    from_first = swap(first, "row", [(r, r ^ 1) for r in range(n_row)])
    from_second = swap(second, ("row", "col"), [(flat(r, c), other(r, c)) for r, c in everyone])

    from_first, tap_weight = lax.optimization_barrier((from_first, tap_weight))
    height = 16 if compact else 48
    tall = span + STEP - 1
    wide = -(-span * tall // LANES) * LANES
    taps, spread, sky = call(
        functools.partial(weights_kernel, height, compact),
        (shape(sectors * STEP, wide), shape(2 * all_cols * height, 2 * LANES), shape(sectors, rows, cols, kind=F32)),
        [tap_weight, tap_sector, far_weight, sky_view],
        [pltpu.VMEM((2 * tall, LANES), F32), pltpu.VMEM((64, LANES), F32)],
        flops=10_000_000,
    )
    def near(at, count):
        return call(
            functools.partial(near_kernel, at),
            shape(count, rows, cols, kind=F32),
            [taps, radiance, side, from_first, from_second, sky],
            [pltpu.VMEM((2, wide, 2 * cols), BF16)],
            flops=2 * sectors * STEP * wide * 2 * cols * count,
        )

    half = bands // 2
    if compact:
        known = first[bands + 1] + from_first[bands + 1]
        theirs = swap(known, "row", [(r, r ^ 2) for r in range(n_row)])
        near_one = near(0, half)
        theirs, near_one = lax.optimization_barrier((theirs, near_one))
        step = 4
        while step < n_row:
            known = known + theirs
            theirs = swap(known, "row", [(r, r ^ step) for r in range(n_row)])
            step *= 2
    else:
        near_one = near(0, half)
        window = coarse_window(radiance, far_reach)
        window = jnp.pad(window, ((0, 0), (0, 0), (0, height - window.shape[2])))
        known = theirs = window.reshape(bands, all_cols * height)
    near_two = near(half, bands - half)
    return call(finish_kernel, shape(bands, rows, cols), [keep, spread, known, theirs, near_one, near_two])


def solution(mesh):
    in_specs = (
        P("slab", "row", "col"),
        P("slab", "row", "col"),
        P(),
        P(),
        P(),
        P(("slab", "row"), "col"),
    )
    out_specs = P("slab", "row", "col")
    return jax.shard_map(body, mesh=mesh, in_specs=in_specs, out_specs=out_specs, check_vma=False)
```

```python
import functools

import jax
import jax.numpy as jnp
from jax import lax
from jax.experimental import pallas as pl
from jax.experimental.pallas import tpu as pltpu
from jax.sharding import PartitionSpec as P

DEC = 16
STEP = 16
LANES = 128
F32 = jnp.float32
BF16 = jnp.bfloat16
I32 = jnp.int32


def iota(shape, axis):
    return lax.broadcasted_iota(I32, shape, axis)


def swap(value, axes, pairs):
    return lax.ppermute(value, axes, pairs)


def shifted(value, axis, steps):
    count = lax.axis_size(axis)
    leading, last = (max(0, -steps), min(count, count - steps))
    return lax.ppermute(value, axis, [(source, source + steps) for source in range(leading, last)])


def fetch_kernel(*refs):
    half = len(refs) // 2
    sems = refs[-1]
    fetches = [pltpu.make_async_copy(refs[k], refs[half + k], sems.at[k]) for k in range(half)]
    for fetch in fetches:
        fetch.start()
    for fetch in fetches:
        fetch.wait()


def pack_kernel(radiance_ref, other_ref, first_ref, second_ref, side_ref):
    row, col = lax.axis_index("row"), lax.axis_index("col")
    bands, rows, cols = radiance_ref.shape
    height = rows // DEC
    known = jnp.zeros((bands, 256), F32)
    own_row = (iota((bands, height, 256), 2) & 15) - iota((bands, height, 256), 1)
    offset = (iota((cols, 256), 1) >> 4) - (iota((cols, 256), 0) >> 4)
    for ref, which in ((radiance_ref, col), (other_ref, 1 - col)):
        chooser = (offset == which * (cols // DEC)).astype(BF16)
        sums = jnp.dot(ref[...].reshape(bands * rows, cols), chooser, preferred_element_type=F32)
        sums = jnp.sum(sums.reshape(bands, height, DEC, 256), axis=2)
        known = known + jnp.sum(jnp.where(own_row == row * height, sums, 0.0), axis=1)
    known = known * (1.0 / (DEC * DEC))
    first_ref[bands + 1] = jnp.concatenate([known[:, :LANES], known[:, LANES:]], axis=0).astype(BF16)
    lane = iota((rows, cols), 1)
    packed = jnp.zeros((rows, cols), F32)
    for b in range(bands):
        moved = pltpu.roll(other_ref[b].astype(F32), 16 * b, 1)
        packed = jnp.where(((lane - (16 * b - 16 * col)) & (cols - 1)) < 16, moved, packed)
    side_ref[...] = packed.astype(BF16)
    odd = row & 1
    near = pl.multiple_of(STEP * (1 - odd), STEP)
    away = pl.multiple_of(STEP * odd, STEP)
    first_ref[0:bands] = radiance_ref[:, pl.ds(near, STEP), :]
    first_ref[bands] = side_ref[pl.ds(near, STEP), :]
    second_ref[0:bands] = radiance_ref[:, pl.ds(away, STEP), :]
    second_ref[bands] = side_ref[pl.ds(away, STEP), :]


def weights_kernel(
    height, whole_grid, tap_ref, sector_ref, far_ref, sky_ref, taps_ref, spread_ref, view_ref, tap_s, far_s
):
    row, col = lax.axis_index("row"), lax.axis_index("col")
    span = tap_ref.shape[0]
    tall = span + STEP - 1
    wide = taps_ref.shape[1]
    sectors = taps_ref.shape[0] // STEP
    tap_s[...] = jnp.zeros(tap_s.shape, F32)
    tap_s[0:span, 0:span] = tap_ref[...]
    tap_s[tall : tall + span, 0:span] = sector_ref[...].astype(F32)
    lane = iota((LANES, wide), 1) - tall * iota((LANES, wide), 0)
    pick = ((lane >= 0) & (lane < tall)).astype(BF16)
    both = jnp.dot(tap_s[...].astype(BF16), pick, preferred_element_type=F32)
    which = iota((tall, wide), 1) % tall == iota((tall, wide), 0)
    weight = jnp.sum(jnp.where(which, both[0:tall], 0.0), axis=0, keepdims=True)
    sector = jnp.sum(jnp.where(which, both[tall:], 0.0), axis=0, keepdims=True)
    weight = pltpu.roll(jnp.broadcast_to(weight, (STEP, wide)), 0, 1, stride=1, stride_axis=0)
    sector = pltpu.roll(jnp.broadcast_to(sector, (STEP, wide)), 0, 1, stride=1, stride_axis=0)
    for s in range(sectors):
        taps_ref[s * STEP : (s + 1) * STEP, :] = jnp.where(sector == s, weight, 0.0).astype(BF16)
    far_s[...] = jnp.zeros(far_s.shape, F32)
    far_s[8 : 8 + span, 0:span] = far_ref[...]
    reach = (span - 1) // 2
    coarse_cols = LANES // DEC
    all_cols = spread_ref.shape[0] // (2 * height)
    lane = iota((LANES, all_cols * LANES), 1)
    want = (lane >> 7) - coarse_cols * col - ((lane & (LANES - 1)) >> 4) + reach
    pick = (iota((LANES, all_cols * LANES), 0) == want).astype(BF16)
    parts = []
    for i in range(2):
        start = (reach - 2 * row if whole_grid else 0) - i + 8
        whole = far_s[pl.ds(start, height), :]
        high = whole.astype(BF16)
        low = (whole - high.astype(F32)).astype(BF16)
        parts += [high.astype(F32), low.astype(F32)]
    stacked = jnp.concatenate(parts, axis=0).astype(BF16)
    moved = jnp.dot(stacked, pick, preferred_element_type=F32).astype(BF16)
    for i in range(2):
        for part in range(2):
            rows = moved[(2 * i + part) * height : (2 * i + part + 1) * height]
            for J in range(all_cols):
                at = (part * all_cols + J) * height
                spread_ref[at : at + height, i * LANES : (i + 1) * LANES] = rows[:, J * LANES : (J + 1) * LANES]
    view_ref[...] = sky_ref[...].astype(F32)


def near_kernel(second, taps_ref, radiance_ref, side_ref, strip_ref, sky_ref, near_ref, tiles):
    row, col, last = lax.axis_index("row"), lax.axis_index("col"), lax.axis_size("row") - 1
    bands, rows, cols = radiance_ref.shape
    sectors = sky_ref.shape[0]
    span = 33
    reach = 16
    tall = STEP + span - 1
    odd = row & 1
    above = (odd == 0) if second else (odd == 1)
    tiles[:, span * tall :, :] = jnp.zeros((2, tiles.shape[1] - span * tall, tiles.shape[2]), BF16)

    def around(b, middle):
        strip = strip_ref[b].astype(F32)
        if second:
            strip = jnp.where(inside, strip, jnp.zeros_like(strip))
        middle = middle.astype(F32)
        upper = jnp.concatenate([strip, middle], axis=0)
        return jnp.where(above, upper, jnp.concatenate([middle, strip], axis=0))

    inside = jnp.where(above, row, last - row) > 0
    packed = around(bands, side_ref[...])
    lane = iota(packed.shape, 1)
    edge = jnp.where(col == 0, (lane < reach).astype(F32), (lane >= cols - reach).astype(F32))
    start = pl.multiple_of(jnp.where(above, 0, STEP), STEP)
    for pair in range(bands // 2):
        slot = pair % 2
        for k in range(2):
            b = 2 * pair + k
            own = around(b, radiance_ref[b])
            aux = pltpu.roll(packed, (cols - 16 * b) % cols, 1) * edge
            for d in range(span):
                shift = d - reach
                if shift > 0:
                    value = jnp.where(lane < shift, aux, own)
                elif shift < 0:
                    value = jnp.where(lane >= cols + shift, aux, own)
                else:
                    value = own
                if shift:
                    value = pltpu.roll(value, (cols - shift) % cols, 1)
                tiles[slot, d * tall : (d + 1) * tall, k * cols : (k + 1) * cols] = value.astype(BF16)
        sums = jnp.dot(taps_ref[...], tiles[slot], preferred_element_type=F32)
        sky = sky_ref[:, pl.ds(start, STEP), :]
        for k in range(2):
            part = sums[:, k * cols : (k + 1) * cols].reshape(sectors, STEP, cols)
            near_ref[2 * pair + k] = jnp.sum(part * sky, axis=0)


def finish_kernel(keep_ref, spread_ref, mine_ref, theirs_ref, one_ref, two_ref, out_ref):
    odd = (lax.axis_index("row") & 1) == 1
    land = keep_ref[0:1, :] > 0
    bands = out_ref.shape[0]
    if mine_ref.shape[0] == 2 * bands:
        known = mine_ref[...].astype(F32) + theirs_ref[...].astype(F32)
        known = jnp.concatenate([known[:bands], known[bands:]], axis=1)
    else:
        known = mine_ref[...].astype(F32)
    known = jnp.concatenate([known, known], axis=1).astype(BF16)
    far = jnp.dot(known, spread_ref[...], preferred_element_type=F32)
    one, two = one_ref[...], two_ref[...]
    for i, near in enumerate((jnp.where(odd, one, two), jnp.where(odd, two, one))):
        total = near + far[:, i * LANES : (i + 1) * LANES][:, None, :]
        out_ref[:, i * DEC : (i + 1) * DEC, :] = jnp.where(land, total, 0.0).astype(BF16)


VMEM = pl.BlockSpec(memory_space=pltpu.VMEM)
SMEM = pl.BlockSpec(memory_space=pltpu.SMEM)
HBM = pl.BlockSpec(memory_space=pltpu.HBM)


def call(kernel, out_shape, operands, scratch=(), flops=0, in_specs=None, vmem=40 << 20):
    moved = sum(a.size * a.dtype.itemsize for a in operands)
    return pl.pallas_call(
        kernel,
        out_shape=out_shape,
        in_specs=in_specs or [VMEM] * len(operands),
        out_specs=jax.tree.map(lambda _: VMEM, out_shape),
        scratch_shapes=list(scratch),
        compiler_params=pltpu.CompilerParams(vmem_limit_bytes=vmem),
        cost_estimate=pl.CostEstimate(flops=flops, bytes_accessed=moved, transcendentals=0),
    )(*operands)


def coarse_window(radiance, reach):
    bands, rows, cols = radiance.shape
    coarse_rows = rows // DEC
    hops = reach // coarse_rows
    live = min(hops, lax.axis_size("row") - 1)
    blocks = radiance.astype(F32).reshape(bands, coarse_rows, DEC, cols // DEC, DEC)
    own = jnp.mean(blocks, axis=(2, 4)).astype(BF16)
    pieces = [jnp.zeros_like(own)] * (2 * hops + 1)
    pieces[hops] = own
    lower = upper = own
    for k in range(1, live + 1):
        lower = shifted(lower, "row", 1)
        upper = shifted(upper, "row", -1)
        pieces[hops - k] = lower
        pieces[hops + k] = upper
    band = jnp.concatenate(pieces, axis=1)
    band = lax.all_gather(band, "col", axis=2, tiled=True)
    return jnp.transpose(band, (0, 2, 1))


def body(radiance, sky_view, tap_weight, tap_sector, far_weight, land_mask):
    bands, rows, cols = radiance.shape
    sectors = sky_view.shape[0]
    span = tap_weight.shape[0]
    far_reach = (far_weight.shape[0] - 1) // 2
    n_row, n_col = lax.axis_size("row"), lax.axis_size("col")
    coarse_rows = rows // DEC
    compact = n_row & (n_row - 1) == 0 and n_row * coarse_rows == 16
    all_cols = n_col * cols // DEC

    def shape(*dims, kind=BF16):
        return jax.ShapeDtypeStruct(dims, kind)

    inputs = [radiance, tap_weight, tap_sector, far_weight]
    other = swap(radiance, "col", [(0, 1), (1, 0)])
    own, tap_weight, tap_sector, far_weight = call(
        fetch_kernel,
        [jax.ShapeDtypeStruct(a.shape, a.dtype) for a in inputs],
        [pltpu.with_memory_space_constraint(a, pltpu.HBM) for a in inputs],
        [pltpu.SemaphoreType.DMA((len(inputs),))],
        in_specs=[HBM] * len(inputs),
    )
    first, second, side = call(
        pack_kernel,
        (
            shape(bands + 2, STEP, LANES),
            shape(bands + 1, STEP, LANES),
            shape(rows, LANES),
        ),
        [own, other],
    )

    def flat(r, c):
        return r * n_col + c

    def beyond(r, c):
        q = r + 1 if r % 2 else r - 1
        return flat(q, c) if 0 <= q < n_row else flat(r, 1 - c)

    everyone = [(r, c) for r in range(n_row) for c in range(n_col)]
    from_first = swap(first, "row", [(r, r ^ 1) for r in range(n_row)])
    from_second = swap(second, ("row", "col"), [(flat(r, c), beyond(r, c)) for r, c in everyone])

    height = 16 if compact else 48
    tall = span + STEP - 1
    wide = -(-span * tall // LANES) * LANES
    taps, spread, sky = call(
        functools.partial(weights_kernel, height, compact),
        (shape(sectors * STEP, wide), shape(2 * all_cols * height, 2 * LANES), shape(sectors, rows, cols, kind=F32)),
        [tap_weight, tap_sector, far_weight, sky_view],
        [pltpu.VMEM((2 * tall, LANES), F32), pltpu.VMEM((64, LANES), F32)],
        flops=10_000_000,
    )
    def near(second, strips):
        return call(
            functools.partial(near_kernel, second),
            shape(bands, STEP, cols, kind=F32),
            [taps, own, side, strips, sky],
            [pltpu.VMEM((2, wide, 2 * cols), BF16)],
            flops=sectors * STEP * wide * 2 * cols * bands,
        )

    keep = jnp.broadcast_to((land_mask[0, 0] > 0).astype(F32), (8, LANES))
    if compact:
        known = first[bands + 1] + from_first[bands + 1]
        theirs = swap(known, "row", [(r, r ^ 2) for r in range(n_row)])
        near_one = near(False, from_first)
        theirs, near_one = lax.optimization_barrier((theirs, near_one))
        step = 4
        while step < n_row:
            known = known + theirs
            theirs = swap(known, "row", [(r, r ^ step) for r in range(n_row)])
            step *= 2
    else:
        near_one = near(False, from_first)
        window = coarse_window(radiance, far_reach)
        window = jnp.pad(window, ((0, 0), (0, 0), (0, height - window.shape[2])))
        known = theirs = window.reshape(bands, all_cols * height)
    near_two = near(True, from_second)
    return call(finish_kernel, shape(bands, rows, cols), [keep, spread, known, theirs, near_one, near_two])


def solution(mesh):
    in_specs = (
        P("slab", "row", "col"),
        P("slab", "row", "col"),
        P(),
        P(),
        P(),
        P(("slab", "row"), "col"),
    )
    out_specs = P("slab", "row", "col")
    return jax.shard_map(body, mesh=mesh, in_specs=in_specs, out_specs=out_specs, check_vma=False)
```

```python
import functools

import jax
import jax.numpy as jnp
from jax import lax
from jax.experimental import pallas as pl
from jax.experimental.pallas import tpu as pltpu
from jax.sharding import PartitionSpec as P

DEC = 16
STEP = 16
LANES = 128
F32 = jnp.float32
BF16 = jnp.bfloat16
I32 = jnp.int32


def iota(shape, axis):
    return lax.broadcasted_iota(I32, shape, axis)


def shifted(value, axis, steps):
    count = lax.axis_size(axis)
    leading, last = (max(0, -steps), min(count, count - steps))
    return lax.ppermute(value, axis, [(source, source + steps) for source in range(leading, last)])


def fetch_kernel(*refs):
    half = len(refs) // 2
    sems = refs[-1]
    fetches = [pltpu.make_async_copy(refs[k], refs[half + k], sems.at[k]) for k in range(half)]
    for fetch in fetches:
        fetch.start()
    for fetch in fetches:
        fetch.wait()


def pack_kernel(radiance_ref, other_ref, first_ref, second_ref, side_ref, corner_s):
    row, col = lax.axis_index("row"), lax.axis_index("col")
    bands, rows, cols = radiance_ref.shape
    height = rows // DEC
    known = jnp.zeros((bands, 256), F32)
    own_row = (iota((bands, height, 256), 2) & 15) - iota((bands, height, 256), 1)
    offset = (iota((cols, 256), 1) >> 4) - (iota((cols, 256), 0) >> 4)
    for ref, which in ((radiance_ref, col), (other_ref, 1 - col)):
        chooser = (offset == which * (cols // DEC)).astype(BF16)
        sums = jnp.dot(ref[...].reshape(bands * rows, cols), chooser, preferred_element_type=F32)
        sums = jnp.sum(sums.reshape(bands, height, DEC, 256), axis=2)
        known = known + jnp.sum(jnp.where(own_row == row * height, sums, 0.0), axis=1)
    known = known * (1.0 / (DEC * DEC))
    first_ref[bands + 1] = jnp.concatenate([known[:, :LANES], known[:, LANES:]], axis=0).astype(BF16)
    lane = iota((rows, cols), 1)

    def edges(ref, side_col):
        packed = jnp.zeros((rows, cols), F32)
        for b in range(bands):
            moved = pltpu.roll(ref[b].astype(F32), 16 * b, 1)
            packed = jnp.where(((lane - (16 * b - 16 * side_col)) & (cols - 1)) < 16, moved, packed)
        return packed.astype(BF16)

    side_ref[...] = edges(other_ref, col)
    corner_s[...] = edges(radiance_ref, 1 - col)
    odd = row & 1
    near = pl.multiple_of(STEP * (1 - odd), STEP)
    away = pl.multiple_of(STEP * odd, STEP)
    first_ref[0:bands] = other_ref[:, pl.ds(near, STEP), :]
    first_ref[bands] = corner_s[pl.ds(near, STEP), :]
    second_ref[0:bands] = other_ref[:, pl.ds(away, STEP), :]
    second_ref[bands] = corner_s[pl.ds(away, STEP), :]


def weights_kernel(
    height, whole_grid, tap_ref, sector_ref, far_ref, sky_ref, taps_ref, spread_ref, view_ref, tap_s, far_s
):
    row, col = lax.axis_index("row"), lax.axis_index("col")
    span = tap_ref.shape[0]
    tall = span + STEP - 1
    wide = taps_ref.shape[1]
    sectors = taps_ref.shape[0] // STEP
    tap_s[...] = jnp.zeros(tap_s.shape, F32)
    tap_s[0:span, 0:span] = tap_ref[...]
    tap_s[tall : tall + span, 0:span] = sector_ref[...].astype(F32)
    lane = iota((LANES, wide), 1) - tall * iota((LANES, wide), 0)
    pick = ((lane >= 0) & (lane < tall)).astype(BF16)
    both = jnp.dot(tap_s[...].astype(BF16), pick, preferred_element_type=F32)
    which = iota((tall, wide), 1) % tall == iota((tall, wide), 0)
    weight = jnp.sum(jnp.where(which, both[0:tall], 0.0), axis=0, keepdims=True)
    sector = jnp.sum(jnp.where(which, both[tall:], 0.0), axis=0, keepdims=True)
    weight = pltpu.roll(jnp.broadcast_to(weight, (STEP, wide)), 0, 1, stride=1, stride_axis=0)
    sector = pltpu.roll(jnp.broadcast_to(sector, (STEP, wide)), 0, 1, stride=1, stride_axis=0)
    for s in range(sectors):
        taps_ref[s * STEP : (s + 1) * STEP, :] = jnp.where(sector == s, weight, 0.0).astype(BF16)
    far_s[...] = jnp.zeros(far_s.shape, F32)
    far_s[8 : 8 + span, 0:span] = far_ref[...]
    reach = (span - 1) // 2
    coarse_cols = LANES // DEC
    all_cols = spread_ref.shape[0] // (2 * height)
    lane = iota((LANES, all_cols * LANES), 1)
    want = (lane >> 7) - coarse_cols * col - ((lane & (LANES - 1)) >> 4) + reach
    pick = (iota((LANES, all_cols * LANES), 0) == want).astype(BF16)
    parts = []
    for i in range(2):
        start = (reach - 2 * row if whole_grid else 0) - i + 8
        whole = far_s[pl.ds(start, height), :]
        high = whole.astype(BF16)
        low = (whole - high.astype(F32)).astype(BF16)
        parts += [high.astype(F32), low.astype(F32)]
    stacked = jnp.concatenate(parts, axis=0).astype(BF16)
    moved = jnp.dot(stacked, pick, preferred_element_type=F32).astype(BF16)
    for i in range(2):
        for part in range(2):
            rows = moved[(2 * i + part) * height : (2 * i + part + 1) * height]
            for J in range(all_cols):
                at = (part * all_cols + J) * height
                spread_ref[at : at + height, i * LANES : (i + 1) * LANES] = rows[:, J * LANES : (J + 1) * LANES]
    view_ref[...] = sky_ref[...].astype(F32)


def near_kernel(second, taps_ref, radiance_ref, side_ref, strip_ref, sky_ref, near_ref, tiles):
    row, col, last = lax.axis_index("row"), lax.axis_index("col"), lax.axis_size("row") - 1
    bands, rows, cols = radiance_ref.shape
    sectors = sky_ref.shape[0]
    span = 33
    reach = 16
    tall = STEP + span - 1
    odd = row & 1
    above = (odd == 0) if second else (odd == 1)
    tiles[:, span * tall :, :] = jnp.zeros((2, tiles.shape[1] - span * tall, tiles.shape[2]), BF16)

    def around(b, middle):
        strip = strip_ref[b].astype(F32)
        if second:
            strip = jnp.where(inside, strip, jnp.zeros_like(strip))
        middle = middle.astype(F32)
        upper = jnp.concatenate([strip, middle], axis=0)
        return jnp.where(above, upper, jnp.concatenate([middle, strip], axis=0))

    inside = jnp.where(above, row, last - row) > 0
    packed = around(bands, side_ref[...])
    lane = iota(packed.shape, 1)
    edge = jnp.where(col == 0, (lane < reach).astype(F32), (lane >= cols - reach).astype(F32))
    start = pl.multiple_of(jnp.where(above, 0, STEP), STEP)
    for pair in range(bands // 2):
        slot = pair % 2
        for k in range(2):
            b = 2 * pair + k
            own = around(b, radiance_ref[b])
            aux = pltpu.roll(packed, (cols - 16 * b) % cols, 1) * edge
            for d in range(span):
                shift = d - reach
                if shift > 0:
                    value = jnp.where(lane < shift, aux, own)
                elif shift < 0:
                    value = jnp.where(lane >= cols + shift, aux, own)
                else:
                    value = own
                if shift:
                    value = pltpu.roll(value, (cols - shift) % cols, 1)
                tiles[slot, d * tall : (d + 1) * tall, k * cols : (k + 1) * cols] = value.astype(BF16)
        sums = jnp.dot(taps_ref[...], tiles[slot], preferred_element_type=F32)
        sky = sky_ref[:, pl.ds(start, STEP), :]
        for k in range(2):
            part = sums[:, k * cols : (k + 1) * cols].reshape(sectors, STEP, cols)
            near_ref[2 * pair + k] = jnp.sum(part * sky, axis=0)


def finish_kernel(keep_ref, spread_ref, mine_ref, theirs_ref, one_ref, two_ref, out_ref):
    odd = (lax.axis_index("row") & 1) == 1
    land = keep_ref[0:1, :] > 0
    bands = out_ref.shape[0]
    if mine_ref.shape[0] == 2 * bands:
        known = mine_ref[...].astype(F32) + theirs_ref[...].astype(F32)
        known = jnp.concatenate([known[:bands], known[bands:]], axis=1)
    else:
        known = mine_ref[...].astype(F32)
    known = jnp.concatenate([known, known], axis=1).astype(BF16)
    far = jnp.dot(known, spread_ref[...], preferred_element_type=F32)
    one, two = one_ref[...], two_ref[...]
    for i, near in enumerate((jnp.where(odd, one, two), jnp.where(odd, two, one))):
        total = near + far[:, i * LANES : (i + 1) * LANES][:, None, :]
        out_ref[:, i * DEC : (i + 1) * DEC, :] = jnp.where(land, total, 0.0).astype(BF16)


VMEM = pl.BlockSpec(memory_space=pltpu.VMEM)
SMEM = pl.BlockSpec(memory_space=pltpu.SMEM)
HBM = pl.BlockSpec(memory_space=pltpu.HBM)


def call(kernel, out_shape, operands, scratch=(), flops=0, in_specs=None, vmem=40 << 20):
    moved = sum(a.size * a.dtype.itemsize for a in operands)
    return pl.pallas_call(
        kernel,
        out_shape=out_shape,
        in_specs=in_specs or [VMEM] * len(operands),
        out_specs=jax.tree.map(lambda _: VMEM, out_shape),
        scratch_shapes=list(scratch),
        compiler_params=pltpu.CompilerParams(vmem_limit_bytes=vmem),
        cost_estimate=pl.CostEstimate(flops=flops, bytes_accessed=moved, transcendentals=0),
    )(*operands)


def coarse_window(radiance, reach):
    bands, rows, cols = radiance.shape
    coarse_rows = rows // DEC
    hops = reach // coarse_rows
    live = min(hops, lax.axis_size("row") - 1)
    blocks = radiance.astype(F32).reshape(bands, coarse_rows, DEC, cols // DEC, DEC)
    own = jnp.mean(blocks, axis=(2, 4)).astype(BF16)
    pieces = [jnp.zeros_like(own)] * (2 * hops + 1)
    pieces[hops] = own
    lower = upper = own
    for k in range(1, live + 1):
        lower = shifted(lower, "row", 1)
        upper = shifted(upper, "row", -1)
        pieces[hops - k] = lower
        pieces[hops + k] = upper
    band = jnp.concatenate(pieces, axis=1)
    band = lax.all_gather(band, "col", axis=2, tiled=True)
    return jnp.transpose(band, (0, 2, 1))


def body(radiance, sky_view, tap_weight, tap_sector, far_weight, land_mask):
    bands, rows, cols = radiance.shape
    sectors = sky_view.shape[0]
    span = tap_weight.shape[0]
    far_reach = (far_weight.shape[0] - 1) // 2
    n_row, n_col = lax.axis_size("row"), lax.axis_size("col")
    coarse_rows = rows // DEC
    compact = n_row & (n_row - 1) == 0 and n_row * coarse_rows == 16
    all_cols = n_col * cols // DEC

    def shape(*dims, kind=BF16):
        return jax.ShapeDtypeStruct(dims, kind)

    inputs = [radiance, tap_weight, tap_sector, far_weight]
    other = lax.ppermute(radiance, "col", [(0, 1), (1, 0)])
    own, tap_weight, tap_sector, far_weight = call(
        fetch_kernel,
        [jax.ShapeDtypeStruct(a.shape, a.dtype) for a in inputs],
        [pltpu.with_memory_space_constraint(a, pltpu.HBM) for a in inputs],
        [pltpu.SemaphoreType.DMA((len(inputs),))],
        in_specs=[HBM] * len(inputs),
    )
    first, second, side = call(
        pack_kernel,
        (
            shape(bands + 2, STEP, LANES),
            shape(bands + 1, STEP, LANES),
            shape(rows, LANES),
        ),
        [own, other],
        [pltpu.VMEM((rows, cols), BF16)],
    )

    everyone = [(r, c) for r in range(n_row) for c in range(n_col)]

    def crossing(value, partner):
        pairs = [(r * n_col + c, partner(r) * n_col + 1 - c) for r, c in everyone]
        return lax.ppermute(value, ("row", "col"), pairs)

    def beyond(r):
        q = r + 1 if r % 2 else r - 1
        return q if 0 <= q < n_row else r

    from_first = crossing(first, lambda r: r ^ 1)
    from_second = crossing(second, beyond)

    height = 16 if compact else 48
    tall = span + STEP - 1
    wide = -(-span * tall // LANES) * LANES
    taps, spread, sky = call(
        functools.partial(weights_kernel, height, compact),
        (shape(sectors * STEP, wide), shape(2 * all_cols * height, 2 * LANES), shape(sectors, rows, cols, kind=F32)),
        [tap_weight, tap_sector, far_weight, sky_view],
        [pltpu.VMEM((2 * tall, LANES), F32), pltpu.VMEM((64, LANES), F32)],
        flops=10_000_000,
    )
    def near(second, strips):
        return call(
            functools.partial(near_kernel, second),
            shape(bands, STEP, cols, kind=F32),
            [taps, own, side, strips, sky],
            [pltpu.VMEM((2, wide, 2 * cols), BF16)],
            flops=sectors * STEP * wide * 2 * cols * bands,
        )

    keep = jnp.broadcast_to((land_mask[0, 0] > 0).astype(F32), (8, LANES))
    if compact:
        known = first[bands + 1] + from_first[bands + 1]
        theirs = crossing(known, lambda r: r ^ 2)
        near_one = near(False, from_first)
        theirs, near_one = lax.optimization_barrier((theirs, near_one))
        step = 4
        while step < n_row:
            known = known + theirs
            theirs = crossing(known, lambda r, k=step: r ^ k)
            step *= 2
    else:
        near_one = near(False, from_first)
        window = coarse_window(radiance, far_reach)
        window = jnp.pad(window, ((0, 0), (0, 0), (0, height - window.shape[2])))
        known = theirs = window.reshape(bands, all_cols * height)
    near_two = near(True, from_second)
    return call(finish_kernel, shape(bands, rows, cols), [keep, spread, known, theirs, near_one, near_two])


def solution(mesh):
    in_specs = (
        P("slab", "row", "col"),
        P("slab", "row", "col"),
        P(),
        P(),
        P(),
        P(("slab", "row"), "col"),
    )
    out_specs = P("slab", "row", "col")
    return jax.shard_map(body, mesh=mesh, in_specs=in_specs, out_specs=out_specs, check_vma=False)
```

```python
import functools

import jax
import jax.numpy as jnp
from jax import lax
from jax.experimental import pallas as pl
from jax.experimental.pallas import tpu as pltpu
from jax.sharding import PartitionSpec as P

DEC = 16
STEP = 16
LANES = 128
F32 = jnp.float32
BF16 = jnp.bfloat16
I32 = jnp.int32


def iota(shape, axis):
    return lax.broadcasted_iota(I32, shape, axis)


def shifted(value, axis, steps):
    count = lax.axis_size(axis)
    leading, last = (max(0, -steps), min(count, count - steps))
    return lax.ppermute(value, axis, [(source, source + steps) for source in range(leading, last)])


def fetch_kernel(*refs):
    half = len(refs) // 2
    sems = refs[-1]
    fetches = [pltpu.make_async_copy(refs[k], refs[half + k], sems.at[k]) for k in range(half)]
    for fetch in fetches:
        fetch.start()
    for fetch in fetches:
        fetch.wait()


def pack_kernel(radiance_ref, other_ref, first_ref, second_ref, side_ref, corner_s):
    row, col = lax.axis_index("row"), lax.axis_index("col")
    bands, rows, cols = radiance_ref.shape
    height = rows // DEC
    known = jnp.zeros((bands, 256), F32)
    own_row = (iota((bands, height, 256), 2) & 15) - iota((bands, height, 256), 1)
    offset = (iota((cols, 256), 1) >> 4) - (iota((cols, 256), 0) >> 4)
    for ref, which in ((radiance_ref, col), (other_ref, 1 - col)):
        chooser = (offset == which * (cols // DEC)).astype(BF16)
        sums = jnp.dot(ref[...].reshape(bands * rows, cols), chooser, preferred_element_type=F32)
        sums = jnp.sum(sums.reshape(bands, height, DEC, 256), axis=2)
        known = known + jnp.sum(jnp.where(own_row == row * height, sums, 0.0), axis=1)
    known = known * (1.0 / (DEC * DEC))
    first_ref[bands + 1] = jnp.concatenate([known[:, :LANES], known[:, LANES:]], axis=0).astype(BF16)
    lane = iota((rows, cols), 1)

    def edges(ref, side_col):
        packed = jnp.zeros((rows, cols), F32)
        for b in range(bands):
            moved = pltpu.roll(ref[b].astype(F32), 16 * b, 1)
            packed = jnp.where(((lane - (16 * b - 16 * side_col)) & (cols - 1)) < 16, moved, packed)
        return packed.astype(BF16)

    side_ref[...] = edges(other_ref, col)
    corner_s[...] = edges(radiance_ref, 1 - col)
    odd = row & 1
    near = pl.multiple_of(STEP * (1 - odd), STEP)
    away = pl.multiple_of(STEP * odd, STEP)
    first_ref[0:bands] = other_ref[:, pl.ds(near, STEP), :]
    first_ref[bands] = corner_s[pl.ds(near, STEP), :]
    second_ref[0:bands] = other_ref[:, pl.ds(away, STEP), :]
    second_ref[bands] = corner_s[pl.ds(away, STEP), :]


def weights_kernel(
    height, whole_grid, tap_ref, sector_ref, far_ref, sky_ref, taps_ref, spread_ref, view_ref, tap_s, turned_s, far_s
):
    row, col = lax.axis_index("row"), lax.axis_index("col")
    span = tap_ref.shape[0]
    tall = span + STEP - 1
    wide = taps_ref.shape[1]
    sectors = taps_ref.shape[0] // STEP
    tap_s[...] = jnp.zeros(tap_s.shape, F32)
    tap_s[0, 0:span, 0:span] = tap_ref[...]
    tap_s[1, 0:span, 0:span] = sector_ref[...].astype(F32)
    lane = iota((STEP, LANES), 1)
    chunks = [[jnp.zeros((STEP, LANES), F32)] * (wide // LANES) for _ in range(2)]
    for which in range(2):
        turned_s[which] = tap_s[which].T
        for d in range(span):
            at = d * tall
            row_d = jnp.broadcast_to(turned_s[which, d : d + 1, :], (STEP, LANES))
            moved = pltpu.roll(row_d, at % LANES, 1, stride=1, stride_axis=0)
            first, last = at // LANES, (at + tall - 1) // LANES
            if first == last:
                inside = (lane >= at % LANES) & (lane < at % LANES + tall)
                chunks[which][first] = jnp.where(inside, moved, chunks[which][first])
            else:
                chunks[which][first] = jnp.where(lane >= at % LANES, moved, chunks[which][first])
                chunks[which][last] = jnp.where(lane < (at + tall) % LANES, moved, chunks[which][last])
    weight = [chunk.astype(BF16) for chunk in chunks[0]]
    sector = [chunk.astype(BF16) for chunk in chunks[1]]
    none = jnp.zeros((STEP, LANES), BF16)
    for s in range(sectors):
        for k in range(wide // LANES):
            tile = jnp.where(sector[k] == jnp.array(s, BF16), weight[k], none)
            taps_ref[s * STEP : (s + 1) * STEP, k * LANES : (k + 1) * LANES] = tile
    far_s[...] = jnp.zeros(far_s.shape, F32)
    far_s[8 : 8 + span, 0:span] = far_ref[...]
    reach = (span - 1) // 2
    coarse_cols = LANES // DEC
    all_cols = spread_ref.shape[0] // (2 * height)
    lane = iota((1, all_cols * LANES), 1)
    want = (lane >> 7) - coarse_cols * col - ((lane & (LANES - 1)) >> 4) + reach
    pick = (iota((LANES, all_cols * LANES), 0) == want).astype(BF16)
    parts = []
    for i in range(2):
        start = (reach - 2 * row if whole_grid else 0) - i + 8
        whole = far_s[pl.ds(start, height), :]
        high = whole.astype(BF16)
        low = (whole - high.astype(F32)).astype(BF16)
        parts += [high.astype(F32), low.astype(F32)]
    stacked = jnp.concatenate(parts, axis=0).astype(BF16)
    moved = jnp.dot(stacked, pick, preferred_element_type=F32).astype(BF16)
    for i in range(2):
        for part in range(2):
            rows = moved[(2 * i + part) * height : (2 * i + part + 1) * height]
            for J in range(all_cols):
                at = (part * all_cols + J) * height
                spread_ref[at : at + height, i * LANES : (i + 1) * LANES] = rows[:, J * LANES : (J + 1) * LANES]
    view_ref[...] = sky_ref[...].astype(F32)


def near_kernel(second, taps_ref, radiance_ref, side_ref, strip_ref, sky_ref, near_ref, tiles):
    row, col, last = lax.axis_index("row"), lax.axis_index("col"), lax.axis_size("row") - 1
    bands, rows, cols = radiance_ref.shape
    sectors = sky_ref.shape[0]
    span = 33
    reach = 16
    tall = STEP + span - 1
    odd = row & 1
    above = (odd == 0) if second else (odd == 1)
    tiles[:, span * tall :, :] = jnp.zeros((2, tiles.shape[1] - span * tall, tiles.shape[2]), BF16)

    def around(b, middle):
        strip = strip_ref[b]
        if second:
            strip = jnp.where(inside, strip, jnp.zeros_like(strip))
        upper = jnp.concatenate([strip, middle], axis=0)
        return jnp.where(above, upper, jnp.concatenate([middle, strip], axis=0))

    inside = jnp.where(above, row, last - row) > 0
    packed = around(bands, side_ref[...])
    lane = iota(packed.shape, 1)
    edge = jnp.where(col == 0, (lane < reach).astype(F32), (lane >= cols - reach).astype(F32)).astype(BF16)
    start = pl.multiple_of(jnp.where(above, 0, STEP), STEP)
    for pair in range(bands // 2):
        slot = pair % 2
        for k in range(2):
            b = 2 * pair + k
            own = around(b, radiance_ref[b])
            aux = pltpu.roll(packed, (cols - 16 * b) % cols, 1) * edge
            for d in range(span):
                shift = d - reach
                if shift > 0:
                    value = jnp.where(lane < shift, aux, own)
                elif shift < 0:
                    value = jnp.where(lane >= cols + shift, aux, own)
                else:
                    value = own
                if shift:
                    value = pltpu.roll(value, (cols - shift) % cols, 1)
                tiles[slot, d * tall : (d + 1) * tall, k * cols : (k + 1) * cols] = value
        sums = jnp.dot(taps_ref[...], tiles[slot], preferred_element_type=F32)
        sky = sky_ref[:, pl.ds(start, STEP), :]
        for k in range(2):
            part = sums[:, k * cols : (k + 1) * cols].reshape(sectors, STEP, cols)
            near_ref[2 * pair + k] = jnp.sum(part * sky, axis=0)


def finish_kernel(keep_ref, spread_ref, mine_ref, theirs_ref, one_ref, two_ref, out_ref):
    odd = (lax.axis_index("row") & 1) == 1
    land = keep_ref[0:1, :] > 0
    bands = out_ref.shape[0]
    if mine_ref.shape[0] == 2 * bands:
        known = mine_ref[...].astype(F32) + theirs_ref[...].astype(F32)
        known = jnp.concatenate([known[:bands], known[bands:]], axis=1)
    else:
        known = mine_ref[...].astype(F32)
    known = jnp.concatenate([known, known], axis=1).astype(BF16)
    far = jnp.dot(known, spread_ref[...], preferred_element_type=F32)
    one, two = one_ref[...], two_ref[...]
    for i, near in enumerate((jnp.where(odd, one, two), jnp.where(odd, two, one))):
        total = near + far[:, i * LANES : (i + 1) * LANES][:, None, :]
        out_ref[:, i * DEC : (i + 1) * DEC, :] = jnp.where(land, total, 0.0).astype(BF16)


VMEM = pl.BlockSpec(memory_space=pltpu.VMEM)
SMEM = pl.BlockSpec(memory_space=pltpu.SMEM)
HBM = pl.BlockSpec(memory_space=pltpu.HBM)


def call(kernel, out_shape, operands, scratch=(), flops=0, in_specs=None, vmem=40 << 20):
    moved = sum(a.size * a.dtype.itemsize for a in operands)
    return pl.pallas_call(
        kernel,
        out_shape=out_shape,
        in_specs=in_specs or [VMEM] * len(operands),
        out_specs=jax.tree.map(lambda _: VMEM, out_shape),
        scratch_shapes=list(scratch),
        compiler_params=pltpu.CompilerParams(vmem_limit_bytes=vmem),
        cost_estimate=pl.CostEstimate(flops=flops, bytes_accessed=moved, transcendentals=0),
    )(*operands)


def coarse_window(radiance, reach):
    bands, rows, cols = radiance.shape
    coarse_rows = rows // DEC
    hops = reach // coarse_rows
    live = min(hops, lax.axis_size("row") - 1)
    blocks = radiance.astype(F32).reshape(bands, coarse_rows, DEC, cols // DEC, DEC)
    own = jnp.mean(blocks, axis=(2, 4)).astype(BF16)
    pieces = [jnp.zeros_like(own)] * (2 * hops + 1)
    pieces[hops] = own
    lower = upper = own
    for k in range(1, live + 1):
        lower = shifted(lower, "row", 1)
        upper = shifted(upper, "row", -1)
        pieces[hops - k] = lower
        pieces[hops + k] = upper
    band = jnp.concatenate(pieces, axis=1)
    band = lax.all_gather(band, "col", axis=2, tiled=True)
    return jnp.transpose(band, (0, 2, 1))


def body(radiance, sky_view, tap_weight, tap_sector, far_weight, land_mask):
    bands, rows, cols = radiance.shape
    sectors = sky_view.shape[0]
    span = tap_weight.shape[0]
    far_reach = (far_weight.shape[0] - 1) // 2
    n_row, n_col = lax.axis_size("row"), lax.axis_size("col")
    coarse_rows = rows // DEC
    compact = n_row & (n_row - 1) == 0 and n_row * coarse_rows == 16
    all_cols = n_col * cols // DEC

    def shape(*dims, kind=BF16):
        return jax.ShapeDtypeStruct(dims, kind)

    inputs = [radiance, tap_weight, tap_sector, far_weight]
    other = lax.ppermute(radiance, "col", [(0, 1), (1, 0)])
    own, tap_weight, tap_sector, far_weight = call(
        fetch_kernel,
        [jax.ShapeDtypeStruct(a.shape, a.dtype) for a in inputs],
        [pltpu.with_memory_space_constraint(a, pltpu.HBM) for a in inputs],
        [pltpu.SemaphoreType.DMA((len(inputs),))],
        in_specs=[HBM] * len(inputs),
    )
    height = 16 if compact else 48
    tall = span + STEP - 1
    wide = -(-span * tall // LANES) * LANES
    taps, spread, sky = call(
        functools.partial(weights_kernel, height, compact),
        (shape(sectors * STEP, wide), shape(2 * all_cols * height, 2 * LANES), shape(sectors, rows, cols, kind=F32)),
        [tap_weight, tap_sector, far_weight, sky_view],
        [pltpu.VMEM((2, LANES, LANES), F32), pltpu.VMEM((2, LANES, LANES), F32), pltpu.VMEM((64, LANES), F32)],
        flops=10_000_000,
    )
    other, taps, spread, sky = lax.optimization_barrier((other, taps, spread, sky))
    first, second, side = call(
        pack_kernel,
        (
            shape(bands + 2, STEP, LANES),
            shape(bands + 1, STEP, LANES),
            shape(rows, LANES),
        ),
        [own, other],
        [pltpu.VMEM((rows, cols), BF16)],
    )

    everyone = [(r, c) for r in range(n_row) for c in range(n_col)]

    def crossing(value, partner):
        pairs = [(r * n_col + c, partner(r) * n_col + 1 - c) for r, c in everyone]
        return lax.ppermute(value, ("row", "col"), pairs)

    def beyond(r):
        q = r + 1 if r % 2 else r - 1
        return q if 0 <= q < n_row else r

    from_first = crossing(first, lambda r: r ^ 1)
    from_second = crossing(second, beyond)

    def near(second, strips):
        return call(
            functools.partial(near_kernel, second),
            shape(bands, STEP, cols, kind=F32),
            [taps, own, side, strips, sky],
            [pltpu.VMEM((2, wide, 2 * cols), BF16)],
            flops=sectors * STEP * wide * 2 * cols * bands,
        )

    keep = jnp.broadcast_to((land_mask[0, 0] > 0).astype(F32), (8, LANES))
    if compact:
        known = first[bands + 1] + from_first[bands + 1]
        theirs = crossing(known, lambda r: r ^ 2)
        near_one = near(False, from_first)
        theirs, near_one = lax.optimization_barrier((theirs, near_one))
        step = 4
        while step < n_row:
            known = known + theirs
            theirs = crossing(known, lambda r, k=step: r ^ k)
            step *= 2
    else:
        near_one = near(False, from_first)
        window = coarse_window(radiance, far_reach)
        window = jnp.pad(window, ((0, 0), (0, 0), (0, height - window.shape[2])))
        known = theirs = window.reshape(bands, all_cols * height)
    near_two = near(True, from_second)
    return call(finish_kernel, shape(bands, rows, cols), [keep, spread, known, theirs, near_one, near_two])


def solution(mesh):
    in_specs = (
        P("slab", "row", "col"),
        P("slab", "row", "col"),
        P(),
        P(),
        P(),
        P(("slab", "row"), "col"),
    )
    out_specs = P("slab", "row", "col")
    return jax.shard_map(body, mesh=mesh, in_specs=in_specs, out_specs=out_specs, check_vma=False)
```
